32 devices in a mesh: rep: 16 (over z, x, core), shard: 2 (over y).
Axes of the slice: x: 2, y: 2, z: 4, core: 2. Of those that a mesh axis runs over, the one named last changes fastest.
Arguments:
- images: bfloat16 [160, 197, 768], P(('rep', 'shard')), may hold values from -6 to 6
- ln1_gain: bfloat16 [768], P('shard'), may hold values from 0.25 to 1.75
- first_norm_bias: bfloat16 [768], P('shard'), may hold values from -3 to 3
- qkv_weight: bfloat16 [768, 2304], P('shard'), may hold values from -0.21875 to 0.21875
- q_bias: bfloat16 [768], P('shard'), may hold values from -3 to 3
- v_bias: bfloat16 [768], P('shard'), may hold values from -3 to 3
- out_weight: bfloat16 [768, 768], P('shard'), may hold values from -1.75 to 1.75
- out_bias: bfloat16 [768], P('shard'), may hold values from -3 to 3
- ln2_gain: bfloat16 [768], P('shard'), may hold values from 0.25 to 1.75
- second_norm_bias: bfloat16 [768], P('shard'), may hold values from -3 to 3
- up_weight: bfloat16 [768, 3072], P('shard'), may hold values from -0.21875 to 0.21875
- up_bias: bfloat16 [3072], P('shard'), may hold values from -3 to 3
- down_weight: bfloat16 [3072, 768], P('shard'), may hold values from -0.109375 to 0.109375
- down_bias: bfloat16 [768], P('shard'), may hold values from -3 to 3
- cotangent: bfloat16 [160, 197, 768], P(('rep', 'shard')), may hold values from -6 to 6
Outputs:
- result: bfloat16 [160, 197, 768], P(('rep', 'shard'))
- grad_images: bfloat16 [160, 197, 768], P(('rep', 'shard'))
- grad_ln1_gain: float32 [768], P('shard')
- grad_ln1_bias: float32 [768], P('shard')
- grad_qkv_weight: float32 [768, 2304], P('shard')
- grad_q_bias: float32 [768], P('shard')
- grad_v_bias: float32 [768], P('shard')
- grad_out_weight: float32 [768, 768], P('shard')
- grad_out_bias: float32 [768], P('shard')
- grad_ln2_gain: float32 [768], P('shard')
- grad_ln2_bias: float32 [768], P('shard')
- grad_up_weight: float32 [768, 3072], P('shard')
- grad_up_bias: float32 [3072], P('shard')
- grad_down_weight: float32 [3072, 768], P('shard')
- grad_down_bias: float32 [768], P('shard')
The draws below stay inside these ranges and needn't reach their ends.
All inputs are finite; a program needn't handle non-finite values.
Results may differ from the reference program's by a relative error of at most 0.012.
Values may be sent and summed in bfloat16 or wider, within the bound.
No kernel may reach another device: no remote copies, remote signals or barrier semaphores. Data moves between devices by JAX's collectives and lax.ppermute only.
A program may use at most 256 MiB of HBM per device.

```python
import math
import jax
import jax.numpy as jnp
from jax import lax

D = 768
HEADS = 12
HEAD = 64
FF = 3072
SEQ = 197
IMAGES = 160


def steps_of(stream_key, extent, pieces, smallest, top_value):
    loudness, own = 1.0, jax.random.fold_in(stream_key, 6)
    for position, parts in pieces:
        steps = jnp.exp(jax.random.uniform(jax.random.fold_in(own, position), (parts,), jnp.float32, smallest / len(pieces), top_value / len(pieces)))
        loudness = loudness * jnp.repeat(steps, extent[position] // parts).reshape([-1 if axis == position else 1 for axis in range(len(extent))])
    return loudness


def noise(rng, shape, width, limit, split=(), kind=jnp.bfloat16):
    drawn = jax.random.normal(rng, shape, jnp.float32) * width
    if len(split) > 0:
        drawn = steps_of(rng, shape, split, -0.22, 0.18) * drawn
    return jnp.clip(drawn, min=-limit, max=limit).astype(kind)


def setup_inputs(seed: int = 0) -> dict:
    key_of = jax.random.split(jax.random.key(seed), 16)
    return {
        "images": noise(key_of[0], (IMAGES, SEQ, D), 1.0, 6.0, ((0, 32),)),
        "ln1_gain": jnp.clip(1.0 + 0.15 * jax.random.normal(key_of[1], (D,), jnp.float32), 0.25, 1.75).astype(jnp.bfloat16),
        "first_norm_bias": noise(key_of[2], (D,), 0.5, 3.0, ((0, 2),)),
        "qkv_weight": noise(key_of[3], (D, 3 * D), D ** -0.5, 0.21875, ((0, 2),)),
        "q_bias": noise(key_of[4], (D,), 0.5, 3.0, ((0, 2),)),
        "v_bias": noise(key_of[5], (D,), 0.5, 3.0, ((0, 2),)),
        "out_weight": noise(key_of[6], (D, D), (D // 64) ** -0.5, 1.75, ((0, 2),)),
        "out_bias": noise(key_of[7], (D,), 0.5, 3.0, ((0, 2),)),
        "ln2_gain": jnp.clip(1.0 + 0.15 * jax.random.normal(key_of[8], (D,), jnp.float32), 0.25, 1.75).astype(jnp.bfloat16),
        "second_norm_bias": noise(key_of[9], (D,), 0.5, 3.0, ((0, 2),)),
        "up_weight": noise(key_of[10], (D, FF), D ** -0.5, 0.21875, ((0, 2),)),
        "up_bias": noise(key_of[11], (FF,), 0.5, 3.0, ((0, 2),)),
        "down_weight": noise(key_of[12], (FF, D), FF ** -0.5, 0.109375, ((0, 2),)),
        "down_bias": noise(key_of[13], (D,), 0.5, 3.0, ((0, 2),)),
        "cotangent": noise(key_of[14], (IMAGES, SEQ, D), 1.0, 6.0, ((0, 32),)),
    }


def matmul(left, right):
    return jnp.dot(left.astype(jnp.float32), right.astype(jnp.float32), preferred_element_type=jnp.float32)

def norm_statistics(token_rows):
    row_average = lax.optimization_barrier(jnp.mean(token_rows, axis=-1, keepdims=True))
    centred = token_rows - row_average
    var = lax.optimization_barrier(jnp.mean(centred * centred, axis=-1, keepdims=True))
    scale_factor = lax.rsqrt(var + 1e-06)
    return (centred * scale_factor, scale_factor)

def norm_backward(normalized_gradient, standardized_input, scale_factor, norm_gain):
    scaled_rows = normalized_gradient * norm_gain
    return scale_factor * (scaled_rows - lax.optimization_barrier(jnp.mean(scaled_rows, axis=-1, keepdims=True)) - standardized_input * lax.optimization_barrier(jnp.mean(scaled_rows * standardized_input, axis=-1, keepdims=True)))

def gelu_parts(pre):
    cdf = 0.5 * (1.0 + lax.erf(pre * 0.7071067811865476))
    dens = jnp.exp(-0.5 * pre * pre) * 0.3989422804014327
    return (pre * cdf, cdf + pre * dens)

def layer_block(block_in, block_cot, params):
    ln1_gain, first_norm_bias, qkv_weight, q_bias, v_bias, out_weight, out_bias, ln2_gain, second_norm_bias, up_weight, up_bias, down_weight, down_bias = params
    count = block_in.shape[0]
    scale = HEAD ** (-0.5)
    single_float = jnp.float32
    token_rows = block_in.reshape(-1, D).astype(single_float)
    first_standardized, first_scale_factor = norm_statistics(token_rows)
    first_norm_gain = ln1_gain.astype(single_float)
    first_normalized = (first_standardized * first_norm_gain + first_norm_bias.astype(single_float)).astype(jnp.bfloat16)
    bias_all = jnp.concatenate([q_bias.astype(single_float), jnp.zeros((D,), single_float), v_bias.astype(single_float)])
    qkv = (matmul(first_normalized, qkv_weight) + bias_all).astype(jnp.bfloat16)
    query = qkv[:, :D].reshape(count, SEQ, HEADS, HEAD).astype(single_float)
    keys = qkv[:, D:2 * D].reshape(count, SEQ, HEADS, HEAD).astype(single_float)
    values = qkv[:, 2 * D:].reshape(count, SEQ, HEADS, HEAD).astype(single_float)
    scores = jnp.einsum('nqhe,nkhe->nhqk', query, keys) * scale
    top = lax.optimization_barrier(jnp.max(scores, axis=-1, keepdims=True))
    total = lax.optimization_barrier(jnp.sum(jnp.exp(scores - top), axis=-1, keepdims=True))
    lse = top + jnp.log(total)
    prob_b = jnp.exp(scores - lse).astype(jnp.bfloat16)
    context = jnp.einsum('nhqk,nkhe->nqhe', prob_b.astype(single_float), values).astype(jnp.bfloat16).reshape(-1, D)
    hidden_activation = token_rows + matmul(context, out_weight) + out_bias.astype(single_float)
    second_standardized, second_scale_factor = norm_statistics(hidden_activation)
    second_norm_gain = ln2_gain.astype(single_float)
    second_normalized = (second_standardized * second_norm_gain + second_norm_bias.astype(single_float)).astype(jnp.bfloat16)
    pre = matmul(second_normalized, up_weight) + up_bias.astype(single_float)
    act, slope = gelu_parts(pre)
    act_b = act.astype(jnp.bfloat16)
    result = (hidden_activation + matmul(act_b, down_weight) + down_bias.astype(single_float)).astype(jnp.bfloat16)
    cot = block_cot.reshape(-1, D)
    cotangent_float32 = cot.astype(single_float)
    g_down_bias = lax.optimization_barrier(jnp.sum(cotangent_float32, axis=0))
    g_down = matmul(act_b.T, cot)
    dpre = matmul(cot, down_weight.T) * slope
    dpre_b = dpre.astype(jnp.bfloat16)
    g_up_bias = lax.optimization_barrier(jnp.sum(dpre, axis=0))
    g_up = matmul(second_normalized.T, dpre_b)
    second_normalized_gradient = matmul(dpre_b, up_weight.T)
    second_norm_gain_gradient = lax.optimization_barrier(jnp.sum(second_normalized_gradient * second_standardized, axis=0))
    g_ln2_bias = lax.optimization_barrier(jnp.sum(second_normalized_gradient, axis=0))
    middle_gradient = cotangent_float32 + norm_backward(second_normalized_gradient, second_standardized, second_scale_factor, second_norm_gain)
    dmiddle_b = middle_gradient.astype(jnp.bfloat16)
    g_out_bias = lax.optimization_barrier(jnp.sum(middle_gradient, axis=0))
    g_out = matmul(context.T, dmiddle_b)
    dcontext = matmul(dmiddle_b, out_weight.T).astype(jnp.bfloat16).reshape(count, SEQ, HEADS, HEAD).astype(single_float)
    again = jnp.einsum('nqhe,nkhe->nhqk', query, keys) * scale
    prob = jnp.exp(again - lse)
    prob_b2 = prob.astype(jnp.bfloat16).astype(single_float)
    dprob = jnp.einsum('nqhe,nkhe->nhqk', dcontext, values)
    dvalue = jnp.einsum('nhqk,nqhe->nkhe', prob_b2, dcontext)
    delta = lax.optimization_barrier(jnp.sum(prob * dprob, axis=-1, keepdims=True))
    dscore = (prob * (dprob - delta) * scale).astype(jnp.bfloat16).astype(single_float)
    dquery = jnp.einsum('nhqk,nkhe->nqhe', dscore, keys).reshape(-1, D)
    dkey = jnp.einsum('nhqk,nqhe->nkhe', dscore, query).reshape(-1, D)
    dvalue = dvalue.reshape(-1, D)
    g_q_bias = lax.optimization_barrier(jnp.sum(dquery, axis=0))
    g_v_bias = lax.optimization_barrier(jnp.sum(dvalue, axis=0))
    dqkv = jnp.concatenate([dquery, dkey, dvalue], axis=1).astype(jnp.bfloat16)
    g_qkv = matmul(first_normalized.T, dqkv)
    first_normalized_gradient = matmul(dqkv, qkv_weight.T)
    first_norm_gain_gradient = lax.optimization_barrier(jnp.sum(first_normalized_gradient * first_standardized, axis=0))
    g_ln1_bias = lax.optimization_barrier(jnp.sum(first_normalized_gradient, axis=0))
    input_gradient = (middle_gradient + norm_backward(first_normalized_gradient, first_standardized, first_scale_factor, first_norm_gain)).astype(jnp.bfloat16)
    grads = (first_norm_gain_gradient, g_ln1_bias, g_qkv, g_q_bias, g_v_bias, g_out, g_out_bias, second_norm_gain_gradient, g_ln2_bias, g_up, g_up_bias, g_down, g_down_bias)
    return (result.reshape(count, SEQ, D), input_gradient.reshape(count, SEQ, D), grads)

def reference(images, ln1_gain, first_norm_bias, qkv_weight, q_bias, v_bias, out_weight, out_bias, ln2_gain, second_norm_bias, up_weight, up_bias, down_weight, down_bias, cotangent):
    params = (ln1_gain, first_norm_bias, qkv_weight, q_bias, v_bias, out_weight, out_bias, ln2_gain, second_norm_bias, up_weight, up_bias, down_weight, down_bias)
    total_images = images.shape[0]
    group = math.gcd(total_images, 16)
    blocks = total_images // group
    split_in = images.reshape(blocks, group, SEQ, D)
    split_cot = cotangent.reshape(blocks, group, SEQ, D)
    start = tuple((jnp.zeros(p.shape, jnp.float32) for p in params))

    def step(carry, pair):
        out_blk, din_blk, grads = layer_block(pair[0], pair[1], params)
        return (tuple((c + g for c, g in zip(carry, grads))), (out_blk, din_blk))
    grads, (outs, dins) = lax.scan(step, start, (split_in, split_cot))
    result = outs.reshape(total_images, SEQ, D)
    grad_images = dins.reshape(total_images, SEQ, D)
    return (result, grad_images, grads[0], grads[1], grads[2], grads[3], grads[4], grads[5], grads[6], grads[7], grads[8], grads[9], grads[10], grads[11], grads[12])
```

```python
import jax
import jax.numpy as jnp
from jax import lax
from jax.sharding import PartitionSpec as P

HEADS = 12


def matmul(left, right):
    return jnp.dot(left, right, preferred_element_type=jnp.float32)


def norm_statistics(token_rows):
    row_average = jnp.mean(token_rows, axis=-1, keepdims=True)
    centred = token_rows - row_average
    var = jnp.mean(centred * centred, axis=-1, keepdims=True)
    scale_factor = lax.rsqrt(var + 1e-06)
    return (centred * scale_factor, scale_factor)


def norm_backward(normalized_gradient, standardized_input, scale_factor, norm_gain):
    scaled_rows = normalized_gradient * norm_gain
    return scale_factor * (
        scaled_rows
        - jnp.mean(scaled_rows, axis=-1, keepdims=True)
        - standardized_input * jnp.mean(scaled_rows * standardized_input, axis=-1, keepdims=True)
    )


def gelu_parts(pre):
    cdf = 0.5 * (1.0 + lax.erf(pre * 0.7071067811865476))
    dens = jnp.exp(-0.5 * pre * pre) * 0.3989422804014327
    return (pre * cdf, cdf + pre * dens)


def swap(array, axis, size, step):
    return lax.ppermute(array, axis, [(i, i ^ step) for i in range(size)])


def pick(array, index, axis=0):
    return lax.dynamic_index_in_dim(array, index, axis, keepdims=False)


def join(mine, theirs, bit):
    low = jnp.where(bit == 0, mine, theirs)
    high = jnp.where(bit == 0, theirs, mine)
    return jnp.concatenate([low, high], axis=0)


def gather_rows(part, rep, core, side):
    halves = part.reshape((2, part.shape[0] // 2) + part.shape[1:])
    direct = swap(pick(halves, core), "shard", 2, 1)
    other = join(direct, swap(direct, "rep", rep, 1), core)
    return join(part, other, side)


def add(kept, received):
    return (kept.astype(jnp.float32) + received.astype(jnp.float32)).astype(jnp.bfloat16)


def reduce_rows(whole, rep, place, side, scatter=True):
    rows = whole.shape[0]
    core = place & 1
    parts = whole.astype(jnp.bfloat16).reshape((2, 2, rows // 4) + whole.shape[1:])
    now = add(pick(parts, core, 1), swap(pick(parts, 1 - core, 1), "rep", rep, 1))
    now = add(pick(now, side), swap(pick(now, 1 - side), "shard", 2, 1))
    steps = []
    step = 2
    while step < rep:
        bit = (place // step) & 1
        if now.shape[0] % 16 == 0:
            parts = now.reshape((2, now.shape[0] // 2) + now.shape[1:])
            now = add(pick(parts, bit), swap(pick(parts, 1 - bit), "rep", rep, step))
            steps.append(step)
        else:
            now = add(now, swap(now, "rep", rep, step))
        step *= 2
    for step in reversed([1] + steps):
        bit = (place // step) & 1
        now = join(now, swap(now, "rep", rep, step), bit)
    return now.astype(jnp.float32)


def reduce_small(whole, rep, place, side):
    now = whole
    step = 1
    while step < rep:
        now = now + swap(now, "rep", rep, step)
        step *= 2
    now = now.reshape((2, now.shape[0] // 2) + now.shape[1:])
    return pick(now, side) + swap(pick(now, 1 - side), "shard", 2, 1)


def per_device(
    images,
    ln1_gain,
    first_norm_bias,
    qkv_weight,
    q_bias,
    v_bias,
    out_weight,
    out_bias,
    ln2_gain,
    second_norm_bias,
    up_weight,
    up_bias,
    down_weight,
    down_bias,
    cotangent,
):
    count, seq, width = images.shape
    heads = HEADS
    head = width // heads
    scale = head ** (-0.5)
    single_float = jnp.float32
    brain_float16 = jnp.bfloat16
    rep = lax.axis_size("rep")
    place = lax.axis_index("rep")
    side = lax.axis_index("shard")
    core = place & 1
    small = (
        ln1_gain,
        first_norm_bias,
        q_bias,
        v_bias,
        out_bias,
        ln2_gain,
        second_norm_bias,
        up_bias,
        down_bias,
    )
    packed = jnp.concatenate(small)
    theirs = swap(packed, "shard", 2, 1)
    low = jnp.where(side == 0, packed, theirs)
    high = jnp.where(side == 0, theirs, packed)
    full = []
    at = 0
    for vector in small:
        size = vector.shape[0]
        full.append(jnp.concatenate([low[at : at + size], high[at : at + size]]))
        at += size
    qkv_full = gather_rows(qkv_weight, rep, core, side)
    out_part, _ = lax.optimization_barrier((out_weight, qkv_full[:8, :128]))
    out_full = gather_rows(out_part, rep, core, side)
    up_part, _ = lax.optimization_barrier((up_weight, out_full[:8, :128]))
    up_full = gather_rows(up_part, rep, core, side)
    down_part, _ = lax.optimization_barrier((down_weight, up_full[:8, :128]))
    down_full = gather_rows(down_part, rep, core, side)
    attention_complete = (full[0], full[1], qkv_full, full[2], full[3], out_full, full[4])
    attention_backward = attention_complete
    first_norm_gain = attention_complete[0].astype(single_float)
    token_rows = images.reshape(-1, width).astype(single_float)
    first_standardized, first_scale_factor = norm_statistics(token_rows)
    first_normalized = (
        first_standardized * first_norm_gain + attention_complete[1].astype(single_float)
    ).astype(brain_float16)
    bias_all = jnp.concatenate(
        [
            attention_complete[3].astype(single_float),
            jnp.zeros((width,), single_float),
            attention_complete[4].astype(single_float),
        ]
    )
    qkv = (matmul(first_normalized, attention_complete[2]) + bias_all).astype(brain_float16)
    query = qkv[:, :width].reshape(count, seq, heads, head)
    keys = qkv[:, width : 2 * width].reshape(count, seq, heads, head)
    values = qkv[:, 2 * width :].reshape(count, seq, heads, head)
    scores = jnp.einsum("nqhe,nkhe->nhqk", query, keys, preferred_element_type=single_float) * scale
    top = jnp.max(scores, axis=-1, keepdims=True)
    total = jnp.sum(jnp.exp(scores - top), axis=-1, keepdims=True)
    lse = top + jnp.log(total)
    prob_b = jnp.exp(scores - lse).astype(brain_float16)
    context = (
        jnp.einsum("nhqk,nkhe->nqhe", prob_b, values, preferred_element_type=single_float)
        .astype(brain_float16)
        .reshape(-1, width)
    )
    hidden_activation = (
        token_rows
        + matmul(context, attention_complete[5])
        + attention_complete[6].astype(single_float)
    )
    perceptron_complete = (full[5], full[6], up_full, full[7], down_full, full[8])
    perceptron_backward = perceptron_complete
    second_norm_gain = perceptron_complete[0].astype(single_float)
    second_standardized, second_scale_factor = norm_statistics(hidden_activation)
    second_normalized = (
        second_standardized * second_norm_gain + perceptron_complete[1].astype(single_float)
    ).astype(brain_float16)
    pre = matmul(second_normalized, perceptron_complete[2]) + perceptron_complete[3].astype(
        single_float
    )
    act, slope = gelu_parts(pre)
    act_b = act.astype(brain_float16)
    result = (
        hidden_activation
        + matmul(act_b, perceptron_complete[4])
        + perceptron_complete[5].astype(single_float)
    ).astype(brain_float16)
    cot = cotangent.reshape(-1, width)
    cotangent_float32 = cot.astype(single_float)
    g_down_bias = jnp.sum(cotangent_float32, axis=0)
    g_down = matmul(act_b.T, cot)
    dpre = matmul(cot, perceptron_backward[4].T) * slope
    dpre_b = dpre.astype(brain_float16)
    g_up_bias = jnp.sum(dpre, axis=0)
    g_up = matmul(second_normalized.T, dpre_b)
    second_normalized_gradient = matmul(dpre_b, perceptron_backward[2].T)
    second_norm_gain_gradient = jnp.sum(second_normalized_gradient * second_standardized, axis=0)
    g_ln2_bias = jnp.sum(second_normalized_gradient, axis=0)
    middle_gradient = cotangent_float32 + norm_backward(
        second_normalized_gradient,
        second_standardized,
        second_scale_factor,
        perceptron_backward[0].astype(single_float),
    )
    mlp_grads = (second_norm_gain_gradient, g_ln2_bias, g_up, g_up_bias, g_down, g_down_bias)
    p_down = reduce_rows(g_down, rep, place, side)
    p_up = reduce_rows(g_up, rep, place, side)
    dmiddle_b = middle_gradient.astype(brain_float16)
    g_out_bias = jnp.sum(middle_gradient, axis=0)
    g_out = matmul(context.T, dmiddle_b)
    dcontext = (
        matmul(dmiddle_b, attention_backward[5].T)
        .astype(brain_float16)
        .reshape(count, seq, heads, head)
    )
    again = jnp.einsum("nqhe,nkhe->nhqk", query, keys, preferred_element_type=single_float) * scale
    prob = jnp.exp(again - lse)
    prob_again = prob.astype(brain_float16)
    dprob = jnp.einsum("nqhe,nkhe->nhqk", dcontext, values, preferred_element_type=single_float)
    dvalue = jnp.einsum(
        "nhqk,nqhe->nkhe", prob_again, dcontext, preferred_element_type=single_float
    ).reshape(-1, width)
    delta = jnp.sum(prob * dprob, axis=-1, keepdims=True)
    dscore = (prob * (dprob - delta) * scale).astype(brain_float16)
    dquery = jnp.einsum(
        "nhqk,nkhe->nqhe", dscore, keys, preferred_element_type=single_float
    ).reshape(-1, width)
    dkey = jnp.einsum(
        "nhqk,nqhe->nkhe", dscore, query, preferred_element_type=single_float
    ).reshape(-1, width)
    g_q_bias = jnp.sum(dquery, axis=0)
    g_v_bias = jnp.sum(dvalue, axis=0)
    dqkv = jnp.concatenate([dquery, dkey, dvalue], axis=1).astype(brain_float16)
    g_qkv = matmul(first_normalized.T, dqkv)
    first_normalized_gradient = matmul(dqkv, attention_backward[2].T)
    first_norm_gain_gradient = jnp.sum(first_normalized_gradient * first_standardized, axis=0)
    g_ln1_bias = jnp.sum(first_normalized_gradient, axis=0)
    input_gradient = (
        middle_gradient
        + norm_backward(
            first_normalized_gradient,
            first_standardized,
            first_scale_factor,
            attention_backward[0].astype(single_float),
        )
    ).astype(brain_float16)
    attn_grads = (
        first_norm_gain_gradient,
        g_ln1_bias,
        g_qkv,
        g_q_bias,
        g_v_bias,
        g_out,
        g_out_bias,
    )
    p_out = reduce_rows(g_out, rep, place, side)
    p_qkv = reduce_rows(g_qkv, rep, place, side)
    vectors = (
        first_norm_gain_gradient,
        g_ln1_bias,
        g_q_bias,
        g_v_bias,
        g_out_bias,
        second_norm_gain_gradient,
        g_ln2_bias,
        g_up_bias,
        g_down_bias,
    )
    packed = jnp.concatenate([v.reshape(2, -1) for v in vectors], axis=1)
    summed = reduce_small(packed, rep, place, side).reshape(-1)
    pieces = []
    at = 0
    for v in vectors:
        size = v.shape[0] // 2
        pieces.append(summed[at : at + size])
        at += size
    p_ln1_gain, p_ln1_bias, p_q_bias, p_v_bias, p_out_bias, p_ln2_gain, p_ln2_bias, p_up_bias, p_down_bias = pieces
    return (
        result.reshape(count, seq, width),
        input_gradient.reshape(count, seq, width),
        p_ln1_gain,
        p_ln1_bias,
        p_qkv,
        p_q_bias,
        p_v_bias,
        p_out,
        p_out_bias,
        p_ln2_gain,
        p_ln2_bias,
        p_up,
        p_up_bias,
        p_down,
        p_down_bias,
    )


def solution(mesh):
    in_specs = (
        P(("rep", "shard"), None, None),
        P("shard"),
        P("shard"),
        P("shard", None),
        P("shard"),
        P("shard"),
        P("shard", None),
        P("shard"),
        P("shard"),
        P("shard"),
        P("shard", None),
        P("shard"),
        P("shard", None),
        P("shard"),
        P(("rep", "shard"), None, None),
    )
    out_specs = (
        P(("rep", "shard"), None, None),
        P(("rep", "shard"), None, None),
        P("shard"),
        P("shard"),
        P("shard", None),
        P("shard"),
        P("shard"),
        P("shard", None),
        P("shard"),
        P("shard"),
        P("shard"),
        P("shard", None),
        P("shard"),
        P("shard", None),
        P("shard"),
    )
    return jax.shard_map(
        per_device, mesh=mesh, in_specs=in_specs, out_specs=out_specs, check_vma=False
    )
```

```python
import functools

import jax
import jax.numpy as jnp
from jax import lax
from jax.experimental import pallas as pl
from jax.experimental.pallas import tpu as pltpu
from jax.sharding import PartitionSpec as P


HEADS = 12
F32 = jnp.float32
BF16 = jnp.bfloat16
VMEM_LIMIT = 60 * 2**20
LANES = 128
ANY = pl.BlockSpec(memory_space=pl.ANY)
SMEM = pl.BlockSpec(memory_space=pltpu.SMEM)


def nn(left, right):
    return jnp.dot(left, right, preferred_element_type=F32)


def nt(left, right):
    return lax.dot_general(left, right, (((1,), (1,)), ((), ())), preferred_element_type=F32)


def tn(left, right):
    return lax.dot_general(left, right, (((0,), (0,)), ((), ())), preferred_element_type=F32)


def normalize(rows):
    centred = rows - jnp.mean(rows, axis=-1, keepdims=True)
    factor = lax.rsqrt(jnp.mean(centred * centred, axis=-1, keepdims=True) + 1e-06)
    return centred * factor, factor


def norm_backward(gradient, standardized, factor, gain):
    scaled = gradient * gain
    return factor * (
        scaled
        - jnp.mean(scaled, axis=-1, keepdims=True)
        - standardized * jnp.mean(scaled * standardized, axis=-1, keepdims=True)
    )


def gelu_parts(pre):
    cdf = 0.5 * (1.0 + lax.erf(pre * 0.7071067811865476))
    dens = jnp.exp(-0.5 * pre * pre) * 0.3989422804014327
    return pre * cdf, cdf + pre * dens


def head_masks(head):
    lane = lax.broadcasted_iota(jnp.int32, (1, LANES), 1)
    return [
        jnp.logical_and(lane >= h * head, lane < (h + 1) * head).astype(BF16)
        for h in range(LANES // head)
    ]


def resident(shape):
    return pl.BlockSpec(
        shape, lambda *_: tuple(0 for _ in shape), pipeline_mode=pl.Buffered(1)
    )


def per_image(shape):
    return pl.BlockSpec(shape, lambda i: (i,) + tuple(0 for _ in shape[1:]))


def params(limit=VMEM_LIMIT):
    return pltpu.CompilerParams(vmem_limit_bytes=limit)


def copy_in(copies):
    for source, target, sem in copies:
        pltpu.make_async_copy(source, target, sem).start()


def wait_in(copies):
    for source, target, sem in copies:
        pltpu.make_async_copy(source, target, sem).wait()


def attention_kernel(
    seq, head, place, images, table, wq_own, wo_own, piece_a, piece_b,
    normed_o, qkv_o, prob_o, context_o, middle_o, normed2_o, wq_o, wo_o,
    rows_s, wq_s, wo_s, sems,
):
    step = pl.program_id(0)
    width = table.shape[1]
    half = width // 2
    quarter = half // 2
    side, core = place[0], place[1]
    base = (1 - side) * half

    def copies():
        mine = pl.multiple_of(side * half, half)
        out = [
            (wq_own, wq_s.at[pl.ds(mine, half), :], sems.at[0]),
            (wo_own, wo_s.at[pl.ds(mine, half), :], sems.at[1]),
        ]
        for n, piece in enumerate((piece_a, piece_b)):
            at = pl.multiple_of(base + (core ^ n) * quarter, quarter)
            rows = pl.ds(at, quarter)
            out.append(
                (piece.at[:, 0 : 3 * width], wq_s.at[rows, :], sems.at[2 + 2 * n])
            )
            out.append(
                (piece.at[:, 3 * width : 4 * width], wo_s.at[rows, :], sems.at[3 + 2 * n])
            )
        return out

    def back():
        return [(wq_s, wq_o, sems.at[6]), (wo_s, wo_o, sems.at[7])]

    @pl.when(step == 0)
    def _():
        copy_in(copies())
        rows_s[...] = jnp.zeros_like(rows_s)

    rows_s[0:seq, :] = images[0].astype(F32)
    rows = rows_s[...]
    standardized, _ = normalize(rows)
    normed = (standardized * table[0:1, :] + table[1:2, :]).astype(BF16)
    normed_o[0] = normed

    @pl.when(step == 0)
    def _():
        wait_in(copies())
        copy_in(back())

    for c in range(3):
        block = nn(normed, wq_s[:, c * width : (c + 1) * width])
        if c == 0:
            block = block + table[2:3, :]
        if c == 2:
            block = block + table[3:4, :]
        qkv_o[0, :, c * width : (c + 1) * width] = block.astype(BF16)

    masks = head_masks(head)
    pad = rows_s.shape[0]
    token = lax.broadcasted_iota(jnp.int32, (pad, 1), 0)
    hidden = jnp.where(token < seq, 0.0, -1e30).astype(F32)
    scale = BF16(head**-0.5)
    for j in range(width // LANES):
        at = j * LANES
        query = qkv_o[0, :, at : at + LANES]
        keys = qkv_o[0, :, width + at : width + at + LANES]
        values = qkv_o[0, :, 2 * width + at : 2 * width + at + LANES]
        total = None
        for h, mask in enumerate(masks):
            scores = nt(keys * (mask * scale), query) + hidden
            powers = jnp.exp(scores - jnp.max(scores, axis=0, keepdims=True))
            prob = (powers * (1.0 / jnp.sum(powers, axis=0, keepdims=True))).astype(BF16)
            prob_o[0, len(masks) * j + h] = prob
            part = tn(prob, values * mask)
            total = part if total is None else total + part
        context_o[0, :, at : at + LANES] = total.astype(BF16)

    middle = rows + nn(context_o[0], wo_s[...]) + table[4:5, :]
    middle_o[0] = middle
    standardized2, _ = normalize(middle)
    normed2_o[0] = (standardized2 * table[5:6, :] + table[6:7, :]).astype(BF16)

    @pl.when(step == pl.num_programs(0) - 1)
    def _():
        wait_in(back())


def attention_forward(place, images, table, weights_in, pad, head):
    count, seq, width = images.shape
    shapes = [
        ((count, pad, width), BF16),
        ((count, pad, 3 * width), BF16),
        ((count, width // head, pad, pad), BF16),
        ((count, pad, width), BF16),
        ((count, pad, width), F32),
        ((count, pad, width), BF16),
    ]
    weights = [((width, 3 * width), BF16), ((width, width), BF16)]
    return pl.pallas_call(
        functools.partial(attention_kernel, seq, head),
        grid=(count,),
        out_shape=tuple(jax.ShapeDtypeStruct(s, t) for s, t in shapes + weights),
        in_specs=[SMEM, per_image((1, seq, width)), resident(table.shape)] + [ANY] * 4,
        out_specs=[per_image((1,) + s[1:]) for s, _ in shapes] + [ANY] * 2,
        scratch_shapes=[
            pltpu.VMEM((pad, width), F32),
            pltpu.VMEM((width, 3 * width), BF16),
            pltpu.VMEM((width, width), BF16),
            pltpu.SemaphoreType.DMA((8,)),
        ],
        compiler_params=params(),
        cost_estimate=pl.CostEstimate(
            flops=18 * 10**9, transcendentals=2 * 10**6, bytes_accessed=30 * 10**6
        ),
        name="attention_forward",
    )(place, images, table, *weights_in)


def slot(target, core, side, across, depth):
    first = jnp.where(core == 0, side, across)
    second = jnp.where(core == 0, across, side)
    return target.at[first, second, depth]


def mlp_kernel(
    part, seq, place, normed2, cotangent, table, up_own, down_own, piece_a, piece_b,
    keep_o, send_o, act_o, dpre_o, bias_o, wu_o, wd_o,
    wu, wd, cot_s, gu_s, gd_s, sems, out_sems,
):
    h = pl.program_id(0)
    count = cotangent.shape[0]
    pad = cot_s.shape[0] // count
    block = wu.shape[2]
    half = up_own.shape[0]
    quarter = half // 2
    side, core, across, depth = place[0], place[1], place[2], place[3]
    base = (1 - side) * half

    def copies(k):
        cols = pl.ds((2 * k + part) * block, block)
        own = pl.multiple_of(side * half, half)
        out = [(up_own.at[:, cols], wu.at[k, pl.ds(own, half), :], sems.at[3 * k])]
        for n, piece in enumerate((piece_a, piece_b)):
            at = pl.multiple_of(base + (core ^ n) * quarter, quarter)
            source = piece.at[k * quarter : (k + 1) * quarter]
            out.append((source, wu.at[k, pl.ds(at, quarter), :], sems.at[3 * k + 1 + n]))
        return out

    def down_copies():
        out = [(down_own.at[pl.ds(part * block, block), :], wd.at[side], sems.at[6])]
        rows = block // 2
        for n, piece in enumerate((piece_a, piece_b)):
            at = pl.multiple_of((core ^ n) * rows, rows)
            source = piece.at[2 * quarter : 2 * quarter + rows]
            out.append((source, wd.at[1 - side, pl.ds(at, rows), :], sems.at[7 + n]))
        return out

    def back(k):
        return [
            (wu.at[k], wu_o.at[k], out_sems.at[4 * k]),
            (wd.at[k], wd_o.at[k], out_sems.at[4 * k + 1]),
        ]

    rows = half // 4

    def up_pieces(target, owner, k):
        out = []
        for y in range(2):
            for z in range(4):
                source = gu_s.at[k, pl.ds(y * half + z * rows, rows), :]
                where = slot(target, owner, y ^ side, k ^ across, z ^ depth)
                out.append((source, where, out_sems.at[4 * k + 2]))
        return out

    def down_pieces(target, owner, k):
        out = []
        for x in range(2):
            for z in range(4):
                source = gd_s.at[k, pl.ds(x * half + z * rows, rows), :]
                where = slot(target, owner, k ^ side, x ^ across, z ^ depth)
                out.append((source, where, out_sems.at[4 * k + 3]))
        return out

    def up_out(k, act):
        @pl.when(core == 0)
        def _():
            act(up_pieces(keep_o, 0, k))

        @pl.when(core == 1)
        def _():
            act(up_pieces(send_o, 0, k))

    def down_out(k, act):
        @pl.when(core == 0)
        def _():
            act(down_pieces(send_o, 1, k))

        @pl.when(core == 1)
        def _():
            act(down_pieces(keep_o, 1, k))

    @pl.when(h == 0)
    def _():
        copy_in(copies(0))
        copy_in(down_copies())
        copy_in(copies(1))
        cot_s[...] = jnp.zeros_like(cot_s)
        for i in range(count):
            cot_s[i * pad : i * pad + seq, :] = cotangent[i]
        wait_in(copies(0))
        wait_in(down_copies())
        copy_in(back(0))

    @pl.when(h == 1)
    def _():
        wait_in(copies(1))
        copy_in(back(1))

    lanes = pl.ds(pl.multiple_of(h * half, half), half)
    row = 8 + 2 * part
    bias = jnp.concatenate([table[row : row + 1, lanes], table[row + 1 : row + 2, lanes]], axis=1)
    act, slope = gelu_parts(nn(normed2[...], wu[h]) + bias)
    act_o[...] = act.astype(BF16)
    dpre = nt(cot_s[...], wd[h]) * slope
    bias_o[h] = jnp.broadcast_to(jnp.sum(dpre, axis=0, keepdims=True), (8, block))
    dpre_o[...] = dpre.astype(BF16)
    gu_s[h] = tn(normed2[...], dpre_o[...]).astype(BF16)
    gd_s[h] = tn(act_o[...], cot_s[...]).astype(BF16)
    for k in range(2):

        @pl.when(h == k)
        def _():
            up_out(k, copy_in)
            down_out(k, copy_in)

    @pl.when(h == 1)
    def _():
        for k in range(2):
            wait_in(back(k))
            up_out(k, wait_in)
            down_out(k, wait_in)


def mlp(part, place, normed2, cotangent, table, weights_in):
    seq = cotangent.shape[1]
    tokens, width = normed2.shape
    block = weights_in[0].shape[1] // 4
    piece = (2, 2, 4, width // 8, block)
    out = [
        (piece, BF16),
        (piece, BF16),
        ((tokens, 2 * block), BF16),
        ((tokens, 2 * block), BF16),
        ((2, 8, block), F32),
        ((2, width, block), BF16),
        ((2, block, width), BF16),
    ]
    columns = pl.BlockSpec((tokens, block), lambda h: (0, h))
    return pl.pallas_call(
        functools.partial(mlp_kernel, part, seq),
        grid=(2,),
        out_shape=tuple(jax.ShapeDtypeStruct(s, t) for s, t in out),
        in_specs=[SMEM, resident(normed2.shape), resident(cotangent.shape), resident(table.shape)]
        + [ANY] * 4,
        out_specs=[ANY, ANY, columns, columns, resident((2, 8, block)), ANY, ANY],
        scratch_shapes=[
            pltpu.VMEM((2, width, block), BF16),
            pltpu.VMEM((2, block, width), BF16),
            pltpu.VMEM((tokens, width), BF16),
            pltpu.VMEM((2, width, block), BF16),
            pltpu.VMEM((2, block, width), BF16),
            pltpu.SemaphoreType.DMA((9,)),
            pltpu.SemaphoreType.DMA((8,)),
        ],
        compiler_params=params(),
        cost_estimate=pl.CostEstimate(
            flops=10 * 10**9, transcendentals=10**6, bytes_accessed=20 * 10**6
        ),
        name="mlp",
    )(place, normed2, cotangent, table, *weights_in)


def norm_kernel(seq, table, middle, cotangent, *refs):
    dpre_a, dpre_b, wu_a, wu_b, dmiddle_o, dmiddle_b_o, sums_o, cot_s = refs

    @pl.when(pl.program_id(0) == 0)
    def _():
        cot_s[...] = jnp.zeros_like(cot_s)
        sums_o[...] = jnp.zeros_like(sums_o)

    cot_s[0:seq, :] = cotangent[0].astype(F32)
    gradient = None
    for dpre, wu in ((dpre_a, wu_a), (dpre_b, wu_b)):
        block = wu.shape[2]
        for k in range(2):
            part = nt(dpre[0, :, k * block : (k + 1) * block], wu[k])
            gradient = part if gradient is None else gradient + part
    standardized, factor = normalize(middle[0])
    cot = cot_s[...]
    dmiddle = cot + norm_backward(gradient, standardized, factor, table[5:6, :])
    dmiddle_o[0] = dmiddle
    dmiddle_b_o[0] = dmiddle.astype(BF16)
    for n, value in enumerate((gradient * standardized, gradient, dmiddle, cot)):
        sums_o[n : n + 1, :] += jnp.sum(value, axis=0, keepdims=True)


def norm_gradient(table, middle, cotangent, dpre, wu):
    count, pad, width = middle.shape
    seq = cotangent.shape[1]
    return pl.pallas_call(
        functools.partial(norm_kernel, seq),
        grid=(count,),
        out_shape=(
            jax.ShapeDtypeStruct(middle.shape, F32),
            jax.ShapeDtypeStruct(middle.shape, BF16),
            jax.ShapeDtypeStruct((8, width), F32),
        ),
        in_specs=[resident(table.shape), per_image((1, pad, width)), per_image((1, seq, width))]
        + [per_image((1,) + d.shape[1:]) for d in dpre]
        + [resident(w.shape) for w in wu],
        out_specs=[per_image((1, pad, width))] * 2 + [resident((8, width))],
        scratch_shapes=[pltpu.VMEM((pad, width), F32)],
        compiler_params=params(),
        cost_estimate=pl.CostEstimate(
            flops=5 * 10**9, transcendentals=0, bytes_accessed=20 * 10**6
        ),
        name="norm_gradient",
    )(table, middle, cotangent, *dpre, *wu)


def result_kernel(seq, table, middle, act_a, act_b, wd_a, wd_b, result_o):
    total = middle[0] + table[7:8, :]
    for act, wd in ((act_a, wd_a), (act_b, wd_b)):
        block = wd.shape[1]
        for k in range(2):
            total = total + nn(act[0, :, k * block : (k + 1) * block], wd[k])
    result_o[0] = total[:seq].astype(BF16)


def layer_result(table, middle, act, wd, seq):
    count, pad, width = middle.shape
    return pl.pallas_call(
        functools.partial(result_kernel, seq),
        grid=(count,),
        out_shape=jax.ShapeDtypeStruct((count, seq, width), BF16),
        in_specs=[resident(table.shape), per_image((1, pad, width))]
        + [per_image((1,) + a.shape[1:]) for a in act]
        + [resident(w.shape) for w in wd],
        out_specs=per_image((1, seq, width)),
        compiler_params=params(),
        cost_estimate=pl.CostEstimate(
            flops=5 * 10**9, transcendentals=0, bytes_accessed=20 * 10**6
        ),
        name="layer_result",
    )(table, middle, *act, *wd)


def backward_kernel(
    call, head, place, normed, query, keys, values, prob, dmiddle_b, wo, *refs
):
    if call == 0:
        context, keep_o, send_o, *refs = refs
    elif call == 1:
        _, _, keep_o, send_o, *refs = refs
    else:
        keep_o, send_o, *refs = refs
    dq_o, dk_o, dv_o, qb_o, vb_o, turned, dcontext_s, dqkv_s, g_s, *refs = refs
    if call == 0:
        go_s, sems = refs
    else:
        (sems,) = refs
    j = pl.program_id(0)
    side, core, across, depth = place[0], place[1], place[2], place[3]
    count = prob.shape[0]
    pad = prob.shape[2]
    width = normed.shape[1]
    half = width // 2
    size = half // 8

    def pieces(source, target, owner, offset, sem):
        out = []
        for y in range(2):
            for x in range(2):
                for z in range(4):
                    at = y * half + x * (half // 2) + z * size
                    where = slot(target, owner, y ^ side, x ^ across, z ^ depth)
                    if call < 2:
                        where = where.at[offset : offset + size]
                    out.append((source.at[at : at + size], where, sem))
        return out

    def route(owner, action, *args):
        @pl.when(core == owner)
        def _():
            action(pieces(args[0], keep_o, owner, *args[1:]))

        @pl.when(core != owner)
        def _():
            action(pieces(args[0], send_o, owner, *args[1:]))

    @pl.when(j == 0)
    def _():
        turned[...] = normed[...].T

    dcontext_s[...] = nt(dmiddle_b[...], wo[...]).astype(BF16)
    masks = head_masks(head)
    scale = BF16(head**-0.5)
    q_sum = jnp.zeros((1, LANES), F32)
    v_sum = jnp.zeros((1, LANES), F32)
    for i in range(count):
        rows = slice(i * pad, (i + 1) * pad)
        q, k, v, dcontext = query[rows, :], keys[rows, :], values[rows, :], dcontext_s[rows, :]
        dq = dk = dv = None
        for h, mask in enumerate(masks):
            prob_b = prob[i, h]
            masked = dcontext * mask
            weight = prob_b.astype(F32)
            weighted = weight * nt(v, masked)
            delta = jnp.sum(weighted, axis=0, keepdims=True)
            dscore = (weighted - weight * delta).astype(BF16)
            dv_h = nn(prob_b, masked)
            dk_h = nn(dscore, q * (mask * scale))
            dq_h = tn(dscore, k * (mask * scale))
            dq, dk, dv = (dq_h, dk_h, dv_h) if h == 0 else (dq + dq_h, dk + dk_h, dv + dv_h)
        q_sum = q_sum + jnp.sum(dq, axis=0, keepdims=True)
        v_sum = v_sum + jnp.sum(dv, axis=0, keepdims=True)
        for n, (value, target) in enumerate(((dq, dq_o), (dk, dk_o), (dv, dv_o))):
            rounded = value.astype(BF16)
            dqkv_s[rows, n * LANES : (n + 1) * LANES] = rounded
            target[rows, :] = rounded
    qb_o[0] = jnp.broadcast_to(q_sum, (8, LANES))
    vb_o[0] = jnp.broadcast_to(v_sum, (8, LANES))
    gradient = nn(turned[...], dqkv_s[...]).astype(BF16)

    for k in range(2):

        @pl.when(j == k)
        def _():
            g_s[k] = gradient
            route(k, copy_in, g_s.at[k], call * size, sems.at[k])

    if call == 0:

        @pl.when(j == 0)
        def _():
            g_out = tn(context[...], dmiddle_b[...]).astype(BF16)
            for c in range(2):
                go_s[c] = g_out[:, c * half : (c + 1) * half]
                route(c, copy_in, go_s.at[c], 2 * size, sems.at[2 + c])

    @pl.when(j == 1)
    def _():
        for k in range(2):
            route(k, wait_in, g_s.at[k], call * size, sems.at[k])
            if call == 0:
                route(k, wait_in, go_s.at[k], 2 * size, sems.at[2 + k])


def attention_backward(call, place, normed, qkv, prob, dmiddle_b, wo, extra, head):
    tokens, width = normed.shape
    count, _, pad, _ = prob.shape
    all_pairs = width // LANES
    begin = 2 * call
    piece = (2, 2, 4, width // 16 * (3 if call < 2 else 1), 3 * LANES)
    out = [(piece, BF16)] * 2 + [((tokens, 2 * LANES), BF16)] * 3
    out += [((2, 8, LANES), F32)] * 2

    def column(c):
        return pl.BlockSpec((tokens, LANES), lambda j: (0, c * all_pairs + begin + j))

    in_specs = [
        SMEM,
        resident(normed.shape),
        column(0),
        column(1),
        column(2),
        pl.BlockSpec((count, LANES // head, pad, pad), lambda j: (0, begin + j, 0, 0)),
        resident(dmiddle_b.shape),
        pl.BlockSpec((LANES, width), lambda j: (begin + j, 0)),
    ]
    aliases = {}
    scratch = [
        pltpu.VMEM((width, tokens), BF16),
        pltpu.VMEM((tokens, LANES), BF16),
        pltpu.VMEM((tokens, 3 * LANES), BF16),
        pltpu.VMEM((2, width, 3 * LANES), BF16),
    ]
    if call == 0:
        in_specs.append(resident(extra[0].shape))
        scratch.append(pltpu.VMEM((2, width, 3 * LANES), BF16))
    if call == 1:
        in_specs += [ANY, ANY]
        aliases = {8: 0, 9: 1}
    scratch.append(pltpu.SemaphoreType.DMA((4,)))
    out_specs = [ANY] * 2
    out_specs += [pl.BlockSpec((tokens, LANES), lambda j: (0, j))] * 3
    out_specs += [pl.BlockSpec((1, 8, LANES), lambda j: (j, 0, 0))] * 2
    return pl.pallas_call(
        functools.partial(backward_kernel, call, head),
        grid=(2,),
        out_shape=tuple(jax.ShapeDtypeStruct(s, t) for s, t in out),
        in_specs=in_specs,
        out_specs=out_specs,
        scratch_shapes=scratch,
        input_output_aliases=aliases,
        compiler_params=params(),
        cost_estimate=pl.CostEstimate(
            flops=6 * 10**9, transcendentals=0, bytes_accessed=10 * 10**6
        ),
        name="attention_backward",
    )(place, normed, qkv, qkv, qkv, prob, dmiddle_b, wo, *extra)


def input_kernel(seq, groups, table, images, dmiddle, wq, *refs):
    blocks, (out_o, sums_o, rows_s) = refs[:-3], refs[-3:]
    step = pl.program_id(0)
    width = table.shape[1]

    @pl.when(step == 0)
    def _():
        rows_s[...] = jnp.zeros_like(rows_s)
        sums_o[...] = jnp.zeros_like(sums_o)

    rows_s[0:seq, :] = images[0].astype(F32)
    standardized, factor = normalize(rows_s[...])
    gradient = None
    for c in range(3):
        at = c * width
        for g in range(groups):
            block = blocks[g * 3 + c]
            cols = block.shape[2]
            part = nt(block[0], wq[:, at : at + cols])
            gradient = part if gradient is None else gradient + part
            at += cols
    out = dmiddle[0] + norm_backward(gradient, standardized, factor, table[0:1, :])
    out_o[0] = out[:seq].astype(BF16)
    sums_o[0:1, :] += jnp.sum(gradient * standardized, axis=0, keepdims=True)
    sums_o[1:2, :] += jnp.sum(gradient, axis=0, keepdims=True)


def input_gradient(table, images, dmiddle, wq, groups):
    count, seq, width = images.shape
    pad = dmiddle.shape[1]
    blocks = [b for g in groups for b in g]
    return pl.pallas_call(
        functools.partial(input_kernel, seq, len(groups)),
        grid=(count,),
        out_shape=(
            jax.ShapeDtypeStruct((count, seq, width), BF16),
            jax.ShapeDtypeStruct((8, width), F32),
        ),
        in_specs=[
            resident(table.shape),
            per_image((1, seq, width)),
            per_image((1, pad, width)),
            resident(wq.shape),
        ]
        + [per_image((1,) + b.shape[1:]) for b in blocks],
        out_specs=[per_image((1, seq, width)), resident((8, width))],
        scratch_shapes=[pltpu.VMEM((pad, width), F32)],
        compiler_params=params(),
        cost_estimate=pl.CostEstimate(
            flops=5 * 10**9, transcendentals=0, bytes_accessed=15 * 10**6
        ),
        name="input_gradient",
    )(table, images, dmiddle, wq, *blocks)


def mlp_out_kernel(place, mine_0, mine_1, other_0, other_1, *refs):
    up_o, down_o = refs[-2:]
    across = place[2]
    for s, (mine, other) in enumerate(((mine_0, other_0), (mine_1, other_1))):

        @pl.when(jnp.logical_and(place[1] == 0, pl.program_id(0) ^ across == s))
        def _():
            up_o[...] = mine[0].astype(F32)
            down_o[...] = other[0].astype(F32)

        @pl.when(jnp.logical_and(place[1] == 1, pl.program_id(0) ^ across == s))
        def _():
            up_o[...] = other[0].astype(F32)
            down_o[...] = mine[0].astype(F32)


def mlp_out(part, place, pieces, earlier):
    _, rows, block = pieces[0].shape
    width = rows * 8
    spec = pl.BlockSpec((1, rows, block), lambda x, z, place: (z ^ place[3], 0, 0))
    shapes = (
        jax.ShapeDtypeStruct((width // 2, 4 * block), F32),
        jax.ShapeDtypeStruct((2 * block, width), F32),
    )
    return pl.pallas_call(
        mlp_out_kernel,
        grid_spec=pltpu.PrefetchScalarGridSpec(
            num_scalar_prefetch=1,
            grid=(2, 4),
            in_specs=[spec] * 4 + [ANY] * len(earlier),
            out_specs=[
                pl.BlockSpec((rows, block), lambda x, z, place: (z, 2 * x + part)),
                pl.BlockSpec((rows, width), lambda x, z, place: (8 * part + 4 * x + z, 0)),
            ],
        ),
        out_shape=shapes,
        input_output_aliases={5 + n: n for n in range(len(earlier))},
        compiler_params=params(),
        name="mlp_out",
    )(place, *pieces, *earlier)


def attention_out_kernel(place, *refs):
    large, small, (qkv_o, out_o) = refs[:4], refs[4:8], refs[8:]
    core, across, depth = place[1], place[2], place[3]
    width = out_o.shape[1]
    half = width // 2
    size = half // 8
    for n in range(2):
        owner = core ^ n
        for s in range(2):
            x = across ^ s
            first, second = large[2 * n + s], small[2 * n + s]
            for t in range(4):
                z = depth ^ t
                rows = pl.ds(pl.multiple_of(x * (half // 2) + z * size, size), size)
                for call in range(3):
                    value = second[t] if call == 2 else first[t, call * size : (call + 1) * size]
                    for c in range(3):
                        col = (2 * call + owner) * LANES + c * width
                        cols = pl.ds(pl.multiple_of(col, LANES), LANES)
                        qkv_o[rows, cols] = value[:, c * LANES : (c + 1) * LANES].astype(F32)
                cols = pl.ds(pl.multiple_of(owner * half, half), half)
                out_o[rows, cols] = first[t, 2 * size : 3 * size].astype(F32)


def attention_out(place, pieces, width):
    shapes = ((width // 2, 3 * width), (width // 2, width))
    return pl.pallas_call(
        attention_out_kernel,
        grid=(1,),
        out_shape=tuple(jax.ShapeDtypeStruct(s, F32) for s in shapes),
        in_specs=[SMEM] + [resident(p.shape) for p in pieces],
        out_specs=[resident(s) for s in shapes],
        compiler_params=params(),
        name="attention_out",
    )(place, *pieces)


def swap(array, axis, step):
    size = lax.axis_size(axis)
    return lax.ppermute(array, axis, [(i, i ^ step) for i in range(size)])


def turn(array, order):
    pairs = []
    for r in range(lax.axis_size("rep")):
        for s in range(2):
            there = 2 * r + (s ^ 1) if (r & 1) == order else 2 * (r ^ 2) + s
            pairs.append((2 * r + s, there))
    return lax.ppermute(array, ("rep", "shard"), pairs)


def pick(array, index, axis=0):
    return lax.dynamic_index_in_dim(array, index, axis, keepdims=False)


def after(value, *earlier):
    return lax.optimization_barrier((value,) + earlier)[0]


def add(*values):
    total = values[0].astype(F32)
    for value in values[1:]:
        total = total + value.astype(F32)
    return total.astype(BF16)


DEPTHS = (8, 4, 12)


def reduce_pieces(keep, send):
    got = swap(send, "rep", 1)
    now = add(keep, got)
    got = turn(now[1], 0)
    now = add(now[0], got)
    got = turn(now[1], 1)
    now = add(now[0], got)
    got = [swap(now[n + 1], "rep", step) for n, step in enumerate(DEPTHS)]
    now = add(now[0], *got)
    step = 16
    while step < lax.axis_size("rep"):
        now = add(now, swap(now, "rep", step))
        step *= 2
    got = [swap(now, "rep", step) for step in DEPTHS]
    mine = jnp.stack([now] + got, axis=0)
    near = swap(mine, "rep", 2)
    return mine, near, swap(mine, "rep", 1), swap(near, "rep", 1)


def reduce_vectors(whole, side):
    now = whole
    step = 1
    while step < lax.axis_size("rep"):
        now = now + swap(now, "rep", step)
        step *= 2
    return pick(now, side) + swap(pick(now, 1 - side), "shard", 1)


def per_device(
    images,
    ln1_gain,
    first_norm_bias,
    qkv_weight,
    q_bias,
    v_bias,
    out_weight,
    out_bias,
    ln2_gain,
    second_norm_bias,
    up_weight,
    up_bias,
    down_weight,
    down_bias,
    cotangent,
):
    count, seq, width = images.shape
    head = width // HEADS
    pad = -(-seq // 16) * 16
    tokens = count * pad
    half = width // 2
    index = lax.axis_index("rep")
    side = lax.axis_index("shard")
    core = index & 1
    across = (index >> 1) & 1
    depth = ((index >> 2) & 1) * 2 + ((index >> 3) & 1)
    place = jnp.stack([side, core, across, depth]).astype(jnp.int32)

    small = jnp.concatenate(
        [
            ln1_gain, first_norm_bias, q_bias, v_bias, out_bias, ln2_gain, second_norm_bias,
            down_bias, up_bias,
        ]
    ).reshape(-1, half)
    small_other = swap(small, "shard", 1)
    first = jnp.concatenate(
        [
            pick(qkv_weight.reshape(2, half // 2, -1), core),
            pick(out_weight.reshape(2, half // 2, -1), core),
        ],
        axis=1,
    )
    first_a = swap(first, "shard", 1)
    first_b = swap(first_a, "rep", 1)
    low = jnp.where(side == 0, small, small_other)
    high = jnp.where(side == 0, small_other, small)
    table = jnp.concatenate([low, high], axis=1).astype(F32)

    block = up_weight.shape[1] // 4
    waves = []
    earlier = first_a
    for part in range(2):
        ups = [
            pick(up_weight[:, c * block : (c + 1) * block].reshape(2, half // 2, block), core)
            for c in (part, 2 + part)
        ]
        rows = down_weight[part * block : (part + 1) * block].reshape(2, block // 2, width)
        mine = jnp.concatenate(ups + [pick(rows, core)], axis=0)
        wave_a = swap(after(mine, earlier), "shard", 1)
        earlier = wave_a
        waves.append((up_weight, down_weight, wave_a, swap(wave_a, "rep", 1)))

    flat = lambda a: a.reshape(tokens, -1)
    deep = lambda a: a.reshape(count, pad, -1)
    normed, qkv, prob, context, middle, normed2, wq, wo = attention_forward(
        place, images, table, (qkv_weight, out_weight, first_a, first_b), pad, head
    )
    normed2 = flat(normed2)
    keep, send, act_a, dpre_a, bias_a, wu_a, wd_a = mlp(
        0, place, normed2, cotangent, table, waves[0]
    )
    mlp_a = reduce_pieces(keep, send)
    keep, send, act_b, dpre_b, bias_b, wu_b, wd_b = mlp(
        1, place, normed2, cotangent, table, waves[1]
    )
    mlp_b = reduce_pieces(keep, send)
    dmiddle, dmiddle_b, sums2 = norm_gradient(
        table, middle, cotangent, (deep(dpre_a), deep(dpre_b)), (wu_a, wu_b)
    )
    dmiddle_b = flat(dmiddle_b)
    normed, qkv, context = flat(normed), flat(qkv), flat(context)
    groups, biases = [], []
    keep = send = None
    for call in range(3):
        extra = ((context,), (keep, send), ())[call]
        keep, send, dq, dk, dv, qb, vb = attention_backward(
            call, place, normed, qkv, prob, dmiddle_b, wo, extra, head
        )
        groups.append((deep(dq), deep(dk), deep(dv)))
        biases.append((qb[:, 0], vb[:, 0]))
        if call == 1:
            attn_a = reduce_pieces(keep, send)
        if call == 2:
            attn_b = reduce_pieces(keep, send)
    grad_images, sums1 = input_gradient(table, images, dmiddle, wq, groups)
    result = layer_result(table, middle, (deep(act_a), deep(act_b)), (wd_a, wd_b), seq)
    sums2 = sums2[0:4]

    outs = mlp_out(0, place, mlp_a, ())
    p_up, p_down = mlp_out(1, place, mlp_b, outs)
    p_qkv, p_out = attention_out(place, attn_a + attn_b, width)

    q_sum = jnp.concatenate([b[0] for b in biases]).reshape(width)
    v_sum = jnp.concatenate([b[1] for b in biases]).reshape(width)
    vectors = jnp.concatenate(
        [
            jnp.concatenate([sums1[0:2], q_sum[None], v_sum[None], sums2], axis=0)
            .reshape(8, 2, half)
            .transpose(1, 0, 2),
            jnp.concatenate([bias_a[:, 0:1], bias_b[:, 0:1]], axis=1).reshape(2, 4, half),
        ],
        axis=1,
    )
    rows = reduce_vectors(vectors, side)
    return (
        result,
        grad_images,
        rows[0],
        rows[1],
        p_qkv,
        rows[2],
        rows[3],
        p_out,
        rows[6],
        rows[4],
        rows[5],
        p_up,
        rows[8:].reshape(-1),
        p_down,
        rows[7],
    )


def solution(mesh):
    in_specs = (
        P(("rep", "shard"), None, None),
        P("shard"),
        P("shard"),
        P("shard", None),
        P("shard"),
        P("shard"),
        P("shard", None),
        P("shard"),
        P("shard"),
        P("shard"),
        P("shard", None),
        P("shard"),
        P("shard", None),
        P("shard"),
        P(("rep", "shard"), None, None),
    )
    out_specs = (
        P(("rep", "shard"), None, None),
        P(("rep", "shard"), None, None),
        P("shard"),
        P("shard"),
        P("shard", None),
        P("shard"),
        P("shard"),
        P("shard", None),
        P("shard"),
        P("shard"),
        P("shard"),
        P("shard", None),
        P("shard"),
        P("shard", None),
        P("shard"),
    )

    return jax.shard_map(
        per_device, mesh=mesh, in_specs=in_specs, out_specs=out_specs, check_vma=False
    )
```

```python
import functools

import jax
import jax.numpy as jnp
from jax import lax
from jax.experimental import pallas as pl
from jax.experimental.pallas import tpu as pltpu
from jax.sharding import PartitionSpec as P


HEADS = 12
F32 = jnp.float32
BF16 = jnp.bfloat16
VMEM_LIMIT = 60 * 2**20
LANES = 128
ANY = pl.BlockSpec(memory_space=pl.ANY)
SMEM = pl.BlockSpec(memory_space=pltpu.SMEM)


def nn(left, right):
    return jnp.dot(left, right, preferred_element_type=F32)


def nt(left, right):
    return lax.dot_general(left, right, (((1,), (1,)), ((), ())), preferred_element_type=F32)


def tn(left, right):
    return lax.dot_general(left, right, (((0,), (0,)), ((), ())), preferred_element_type=F32)


def normalize(rows):
    centred = rows - jnp.mean(rows, axis=-1, keepdims=True)
    factor = lax.rsqrt(jnp.mean(centred * centred, axis=-1, keepdims=True) + 1e-06)
    return centred * factor, factor


def norm_backward(gradient, standardized, factor, gain):
    scaled = gradient * gain
    return factor * (
        scaled
        - jnp.mean(scaled, axis=-1, keepdims=True)
        - standardized * jnp.mean(scaled * standardized, axis=-1, keepdims=True)
    )


def gelu_parts(pre):
    cdf = 0.5 * (1.0 + lax.erf(pre * 0.7071067811865476))
    dens = jnp.exp(-0.5 * pre * pre) * 0.3989422804014327
    return pre * cdf, cdf + pre * dens


def head_masks(head):
    lane = lax.broadcasted_iota(jnp.int32, (1, LANES), 1)
    return [
        jnp.logical_and(lane >= h * head, lane < (h + 1) * head).astype(BF16)
        for h in range(LANES // head)
    ]


def resident(shape):
    return pl.BlockSpec(
        shape, lambda *_: tuple(0 for _ in shape), pipeline_mode=pl.Buffered(1)
    )


def per_image(shape):
    return pl.BlockSpec(shape, lambda i: (i,) + tuple(0 for _ in shape[1:]))


def params(limit=VMEM_LIMIT):
    return pltpu.CompilerParams(vmem_limit_bytes=limit)


def copy_in(copies):
    for source, target, sem in copies:
        pltpu.make_async_copy(source, target, sem).start()


def wait_in(copies):
    for source, target, sem in copies:
        pltpu.make_async_copy(source, target, sem).wait()


def attention_kernel(
    seq, head, place, images, cotangent, table, wq_own, wo_own, piece_a, piece_b,
    normed_o, qkv_o, prob_o, context_o, middle_o, normed2_o, padded_o, wq_o, wo_o,
    rows_s, wq_s, wo_s, sems,
):
    step = pl.program_id(0)
    width = table.shape[1]
    half = width // 2
    quarter = half // 2
    side, core = place[0], place[1]
    base = (1 - side) * half

    def copies():
        mine = pl.multiple_of(side * half, half)
        out = [
            (wq_own, wq_s.at[pl.ds(mine, half), :], sems.at[0]),
            (wo_own, wo_s.at[pl.ds(mine, half), :], sems.at[1]),
        ]
        for n, piece in enumerate((piece_a, piece_b)):
            at = pl.multiple_of(base + (core ^ n) * quarter, quarter)
            rows = pl.ds(at, quarter)
            out.append(
                (piece.at[:, 0 : 3 * width], wq_s.at[rows, :], sems.at[2 + 2 * n])
            )
            out.append(
                (piece.at[:, 3 * width : 4 * width], wo_s.at[rows, :], sems.at[3 + 2 * n])
            )
        return out

    def back():
        return [(wq_s, wq_o, sems.at[6]), (wo_s, wo_o, sems.at[7])]

    @pl.when(step == 0)
    def _():
        copy_in(copies())
        rows_s[...] = jnp.zeros_like(rows_s)

    padded_o[0] = jnp.zeros(padded_o.shape[1:], BF16)
    padded_o[0, 0:seq, :] = cotangent[0]
    rows_s[0:seq, :] = images[0].astype(F32)
    rows = rows_s[...]
    standardized, _ = normalize(rows)
    normed = (standardized * table[0:1, :] + table[1:2, :]).astype(BF16)
    normed_o[0] = normed

    @pl.when(step == 0)
    def _():
        wait_in(copies())
        copy_in(back())

    for c in range(3):
        block = nn(normed, wq_s[:, c * width : (c + 1) * width])
        if c == 0:
            block = block + table[2:3, :]
        if c == 2:
            block = block + table[3:4, :]
        qkv_o[0, :, c * width : (c + 1) * width] = block.astype(BF16)

    masks = head_masks(head)
    pad = rows_s.shape[0]
    token = lax.broadcasted_iota(jnp.int32, (pad, 1), 0)
    hidden = jnp.where(token < seq, 0.0, -1e30).astype(F32)
    scale = BF16(head**-0.5)
    for j in range(width // LANES):
        at = j * LANES
        query = qkv_o[0, :, at : at + LANES]
        keys = qkv_o[0, :, width + at : width + at + LANES]
        values = qkv_o[0, :, 2 * width + at : 2 * width + at + LANES]
        total = None
        for h, mask in enumerate(masks):
            scores = nt(keys * (mask * scale), query) + hidden
            powers = jnp.exp(scores - jnp.max(scores, axis=0, keepdims=True))
            prob = (powers * (1.0 / jnp.sum(powers, axis=0, keepdims=True))).astype(BF16)
            prob_o[0, len(masks) * j + h] = prob
            part = tn(prob, values * mask)
            total = part if total is None else total + part
        context_o[0, :, at : at + LANES] = total.astype(BF16)

    middle = rows + nn(context_o[0], wo_s[...]) + table[4:5, :]
    middle_o[0] = middle
    standardized2, _ = normalize(middle)
    normed2_o[0] = (standardized2 * table[5:6, :] + table[6:7, :]).astype(BF16)

    @pl.when(step == pl.num_programs(0) - 1)
    def _():
        wait_in(back())


def attention_forward(place, images, cotangent, table, weights_in, pad, head):
    count, seq, width = images.shape
    shapes = [
        ((count, pad, width), BF16),
        ((count, pad, 3 * width), BF16),
        ((count, width // head, pad, pad), BF16),
        ((count, pad, width), BF16),
        ((count, pad, width), F32),
        ((count, pad, width), BF16),
        ((count, pad, width), BF16),
    ]
    weights = [((width, 3 * width), BF16), ((width, width), BF16)]
    return pl.pallas_call(
        functools.partial(attention_kernel, seq, head),
        grid=(count,),
        out_shape=tuple(jax.ShapeDtypeStruct(s, t) for s, t in shapes + weights),
        in_specs=[SMEM]
        + [per_image((1, seq, width))] * 2
        + [resident(table.shape)]
        + [ANY] * 4,
        out_specs=[per_image((1,) + s[1:]) for s, _ in shapes] + [ANY] * 2,
        scratch_shapes=[
            pltpu.VMEM((pad, width), F32),
            pltpu.VMEM((width, 3 * width), BF16),
            pltpu.VMEM((width, width), BF16),
            pltpu.SemaphoreType.DMA((8,)),
        ],
        compiler_params=params(),
        cost_estimate=pl.CostEstimate(
            flops=18 * 10**9, transcendentals=2 * 10**6, bytes_accessed=30 * 10**6
        ),
        name="attention_forward",
    )(place, images, cotangent, table, *weights_in)


def slot(target, owner, side, across):
    first = jnp.where(owner == 0, side, across)
    second = jnp.where(owner == 0, across, side)
    return target.at[first, second]


def send_out(pieces, core, owner, keep, send, sem):
    @pl.when(core == owner)
    def _():
        for source, where in pieces(keep):
            pltpu.make_async_copy(source, where, sem).start()

    @pl.when(core != owner)
    def _():
        for source, where in pieces(send):
            pltpu.make_async_copy(source, where, sem).start()


def drain(ref, sem):
    pltpu.make_async_copy(ref, ref, sem).wait()


def mlp_kernel(
    part, seq, place, normed2, cotangent, table, up_own, down_own, piece_a, piece_b, middle, *refs
):
    if part == 0:
        (keep_o, send_o, bias_o, r_o, d_o,
         wu, wd, gu_s, gd_s, turned, act_s, dpre_s, r_acc, d_acc, sems, out_sems) = refs
    else:
        (r_in, d_in, keep_o, send_o, bias_o, result_o, dmiddle_o, dmiddle_b_o, sums_o,
         wu, wd, gu_s, gd_s, turned, act_s, dpre_s, r_acc, d_acc, sems, out_sems,
         result_s, dmiddle_s, dmiddle_b_s, middle_s, r_s, d_s) = refs
    h = pl.program_id(0)
    tokens = normed2.shape[0]
    block = wu.shape[2]
    half = up_own.shape[0]
    width = 2 * half
    quarter = half // 2
    side, core, across = place[0], place[1], place[2]
    base = (1 - side) * half

    def copies(k):
        cols = pl.ds((2 * k + part) * block, block)
        own = pl.multiple_of(side * half, half)
        out = [(up_own.at[:, cols], wu.at[k, pl.ds(own, half), :], sems.at[3 * k])]
        for n, piece in enumerate((piece_a, piece_b)):
            at = pl.multiple_of(base + (core ^ n) * quarter, quarter)
            source = piece.at[k * quarter : (k + 1) * quarter]
            out.append((source, wu.at[k, pl.ds(at, quarter), :], sems.at[3 * k + 1 + n]))
        return out

    def down_copies():
        out = [(down_own.at[pl.ds(part * block, block), :], wd.at[side], sems.at[6])]
        rows = block // 2
        for n, piece in enumerate((piece_a, piece_b)):
            at = pl.multiple_of((core ^ n) * rows, rows)
            source = piece.at[2 * quarter : 2 * quarter + rows]
            out.append((source, wd.at[1 - side, pl.ds(at, rows), :], sems.at[7 + n]))
        return out

    def carried():
        return [
            (r_in, r_s, out_sems.at[2]),
            (d_in, d_s, out_sems.at[3]),
            (middle, middle_s, out_sems.at[4]),
        ]

    def up_pieces(target):
        return [(gu_s.at[h, y], slot(target, 0, y ^ side, h ^ across)) for y in range(2)]

    def down_pieces(target):
        return [(gd_s.at[h, x], slot(target, 1, h ^ side, x ^ across)) for x in range(2)]

    @pl.when(h == 0)
    def _():
        copy_in(copies(0))
        copy_in(down_copies())
        copy_in(copies(1))
        if part == 1:
            copy_in(carried())
        turned[...] = normed2[...].T
        wait_in(copies(0))
        wait_in(down_copies())

    @pl.when(h == 1)
    def _():
        wait_in(copies(1))

    lanes = pl.ds(pl.multiple_of(h * half, half), half)
    row = 8 + 2 * part
    bias = jnp.concatenate([table[row : row + 1, lanes], table[row + 1 : row + 2, lanes]], axis=1)
    act, slope = gelu_parts(nn(normed2[...], wu[h]) + bias)
    act_b = act.astype(BF16)
    act_s[...] = act_b
    r_acc[...] = jnp.where(h == 0, 0.0, r_acc[...]) + nn(act_b, wd[h])
    dpre = nt(cotangent[...], wd[h]) * slope
    bias_o[h] = jnp.broadcast_to(jnp.sum(dpre, axis=0, keepdims=True), (8, block))
    dpre_b = dpre.astype(BF16)
    dpre_s[...] = dpre_b
    d_acc[...] = jnp.where(h == 0, 0.0, d_acc[...]) + nt(dpre_b, wu[h])

    @pl.when(h == 1)
    def _():
        if part == 0:
            copy_in([(r_acc, r_o, out_sems.at[2]), (d_acc, d_o, out_sems.at[3])])
            return
        wait_in(carried())
        pad = tokens // result_o.shape[0]

        def image(i, sums):
            rows = pl.ds(pl.multiple_of(i * pad, pad), pad)
            middle_i = middle_s[rows, :]
            result = middle_i + r_s[rows, :] + r_acc[rows, :] + table[7:8, :]
            result_s[i] = result[:seq].astype(BF16)
            standardized, factor = normalize(middle_i)
            gradient = d_s[rows, :] + d_acc[rows, :]
            cot = cotangent[rows, :].astype(F32)
            dmiddle = cot + norm_backward(gradient, standardized, factor, table[5:6, :])
            dmiddle_s[rows, :] = dmiddle
            dmiddle_b_s[rows, :] = dmiddle.astype(BF16)
            copy_in(
                [
                    (result_s.at[i], result_o.at[i], out_sems.at[2]),
                    (dmiddle_s.at[rows, :], dmiddle_o.at[rows, :], out_sems.at[3]),
                    (dmiddle_b_s.at[rows, :], dmiddle_b_o.at[rows, :], out_sems.at[4]),
                ]
            )
            values = (gradient * standardized, gradient, dmiddle, cot)
            return tuple(
                total + jnp.sum(value, axis=0, keepdims=True) for total, value in zip(sums, values)
            )

        zero = jnp.zeros((1, width), F32)
        sums = lax.fori_loop(0, result_o.shape[0], image, (zero,) * 4)
        for n in range(4):
            sums_o[n : n + 1, :] = sums[n]

    gu_s[h] = nn(turned[...], dpre_s[...]).astype(BF16).reshape(gu_s.shape[1:])
    gd_s[h] = tn(act_s[...], cotangent[...]).astype(BF16).reshape(gd_s.shape[1:])
    send_out(up_pieces, core, 0, keep_o, send_o, out_sems.at[0])
    send_out(down_pieces, core, 1, keep_o, send_o, out_sems.at[1])

    @pl.when(h == 1)
    def _():
        if part == 0:
            drain(r_acc, out_sems.at[2])
            drain(d_acc, out_sems.at[3])
        else:
            drain(result_s, out_sems.at[2])
            drain(dmiddle_s, out_sems.at[3])
            drain(dmiddle_b_s, out_sems.at[4])
        drain(gu_s, out_sems.at[0])
        drain(gd_s, out_sems.at[1])


def mlp(part, place, normed2, cotangent, table, weights_in, middle, extra, count, seq):
    tokens, width = normed2.shape
    block = weights_in[0].shape[1] // 4
    piece = (2, 2, 4, width // 8, block)
    out = [(piece, BF16), (piece, BF16), ((2, 8, block), F32)]
    out_specs = [ANY, ANY, resident((2, 8, block))]
    scratch = [
        pltpu.VMEM((2, width, block), BF16),
        pltpu.VMEM((2, block, width), BF16),
        pltpu.VMEM((2, 2, 4, width // 8, block), BF16),
        pltpu.VMEM((2, 2, 4, block // 8, width), BF16),
        pltpu.VMEM((width, tokens), BF16),
        pltpu.VMEM((tokens, block), BF16),
        pltpu.VMEM((tokens, block), BF16),
        pltpu.VMEM((tokens, width), F32),
        pltpu.VMEM((tokens, width), F32),
        pltpu.SemaphoreType.DMA((9,)),
        pltpu.SemaphoreType.DMA((5,)),
    ]
    if part == 0:
        out += [((tokens, width), F32)] * 2
        out_specs += [ANY] * 2
    else:
        out += [
            ((count, seq, width), BF16),
            ((tokens, width), F32),
            ((tokens, width), BF16),
            ((4, width), F32),
        ]
        out_specs += [ANY] * 3 + [resident((4, width))]
        scratch += [
            pltpu.VMEM((count, seq, width), BF16),
            pltpu.VMEM((tokens, width), F32),
            pltpu.VMEM((tokens, width), BF16),
            pltpu.VMEM((tokens, width), F32),
            pltpu.VMEM((tokens, width), F32),
            pltpu.VMEM((tokens, width), F32),
        ]
    return pl.pallas_call(
        functools.partial(mlp_kernel, part, seq),
        grid=(2,),
        out_shape=tuple(jax.ShapeDtypeStruct(s, t) for s, t in out),
        in_specs=[SMEM, resident(normed2.shape), resident(cotangent.shape), resident(table.shape)]
        + [ANY] * (5 + len(extra)),
        out_specs=out_specs,
        scratch_shapes=scratch,
        compiler_params=params(),
        cost_estimate=pl.CostEstimate(
            flops=15 * 10**9, transcendentals=10**6, bytes_accessed=20 * 10**6
        ),
        name="mlp",
    )(place, normed2, cotangent, table, *weights_in, middle, *extra)


def backward_kernel(
    call, head, place, normed, query, keys, values, prob, dmiddle_b, wo, *refs
):
    if call == 0:
        context, *refs = refs
    else:
        refs = refs[3 + 2 * (call == 1) :]
    keep_o, send_o, dq_o, dk_o, dv_o, sums_o, turned, dcontext_s, dqkv_s, g_s, *refs = refs
    if call == 0:
        go_s, sems = refs
    else:
        (sems,) = refs
    j = pl.program_id(0)
    side, core, across = place[0], place[1], place[2]
    count = prob.shape[0]
    pad = prob.shape[2]
    width = normed.shape[1]
    half = width // 2
    size = half // 8

    def route(buffer, owner, offset, sem):
        def pieces(target):
            out = []
            for y in range(2):
                for x in range(2):
                    where = slot(target, owner, y ^ side, x ^ across)
                    if call < 2:
                        where = where.at[:, offset : offset + size]
                    out.append((buffer.at[owner, y, x], where))
            return out

        send_out(pieces, core, owner, keep_o, send_o, sem)

    @pl.when(j == 0)
    def _():
        turned[...] = normed[...].T

    dcontext_s[...] = nt(dmiddle_b[...], wo[...]).astype(BF16)
    masks = head_masks(head)
    scale = BF16(head**-0.5)
    q_sum = jnp.zeros((1, LANES), F32)
    v_sum = jnp.zeros((1, LANES), F32)
    for i in range(count):
        rows = slice(i * pad, (i + 1) * pad)
        q, k, v, dcontext = query[rows, :], keys[rows, :], values[rows, :], dcontext_s[rows, :]
        dq = dk = dv = None
        for h, mask in enumerate(masks):
            prob_b = prob[i, h]
            masked = dcontext * mask
            weight = prob_b.astype(F32)
            weighted = weight * nt(v, masked)
            delta = jnp.sum(weighted, axis=0, keepdims=True)
            dscore = (weighted - weight * delta).astype(BF16)
            dv_h = nn(prob_b, masked)
            dk_h = nn(dscore, q * (mask * scale))
            dq_h = tn(dscore, k * (mask * scale))
            dq, dk, dv = (dq_h, dk_h, dv_h) if h == 0 else (dq + dq_h, dk + dk_h, dv + dv_h)
        q_sum = q_sum + jnp.sum(dq, axis=0, keepdims=True)
        v_sum = v_sum + jnp.sum(dv, axis=0, keepdims=True)
        for n, (value, target) in enumerate(((dq, dq_o), (dk, dk_o), (dv, dv_o))):
            rounded = value.astype(BF16)
            dqkv_s[rows, n * LANES : (n + 1) * LANES] = rounded
            target[rows, :] = rounded
    sums_o[0] = jnp.concatenate([q_sum, v_sum, jnp.zeros((6, LANES), F32)], axis=0)
    g_s[j] = nn(turned[...], dqkv_s[...]).astype(BF16).reshape(g_s.shape[1:])
    route(g_s, j, call * size, sems.at[0])

    if call == 0:

        @pl.when(j == 0)
        def _():
            @pl.loop(0, 2)
            def _(y):
                rows = pl.ds(pl.multiple_of(y * half, half), half)
                g_out = tn(context[:, rows], dmiddle_b[...]).astype(BF16)
                for c in range(2):
                    part = g_out[:, c * half : (c + 1) * half]
                    go_s[c, y] = part.reshape(go_s.shape[2:])

            for c in range(2):
                route(go_s, c, 2 * size, sems.at[1])

    @pl.when(j == 1)
    def _():
        drain(g_s, sems.at[0])
        if call == 0:
            drain(go_s, sems.at[1])


def attention_backward(call, place, normed, qkv, prob, dmiddle_b, wo, context, kept, dqkv, head):
    tokens, width = normed.shape
    count, _, pad, _ = prob.shape
    all_pairs = width // LANES
    begin = 2 * call
    piece = (2, 2, 4, width // 16 * (3 if call < 2 else 1), 3 * LANES)
    out = [(piece, BF16)] * 2 + [((tokens, width), BF16)] * 3 + [((2, 8, LANES), F32)]

    def column(c):
        return pl.BlockSpec((tokens, LANES), lambda j: (0, c * all_pairs + begin + j))

    in_specs = [
        SMEM,
        resident(normed.shape),
        column(0),
        column(1),
        column(2),
        pl.BlockSpec((count, LANES // head, pad, pad), lambda j: (0, begin + j, 0, 0)),
        resident(dmiddle_b.shape),
        pl.BlockSpec((LANES, width), lambda j: (begin + j, 0)),
    ]
    scratch = [
        pltpu.VMEM((width, tokens), BF16),
        pltpu.VMEM((tokens, LANES), BF16),
        pltpu.VMEM((tokens, 3 * LANES), BF16),
        pltpu.VMEM((2, 2, 2, 4, width // 16, 3 * LANES), BF16),
    ]
    aliases = {}
    if call == 0:
        extra = (context,)
        in_specs.append(resident(context.shape))
        scratch.append(pltpu.VMEM((2, 2, 2, 4, width // 16, 3 * LANES), BF16))
    else:
        extra = tuple(dqkv) + (tuple(kept) if call == 1 else ())
        in_specs += [ANY] * len(extra)
        aliases = {8: 2, 9: 3, 10: 4}
        if call == 1:
            aliases.update({11: 0, 12: 1})
    scratch.append(pltpu.SemaphoreType.DMA((2,)))
    out_specs = [ANY] * 2
    out_specs += [pl.BlockSpec((tokens, LANES), lambda j: (0, begin + j))] * 3
    out_specs.append(pl.BlockSpec((1, 8, LANES), lambda j: (j, 0, 0)))
    return pl.pallas_call(
        functools.partial(backward_kernel, call, head),
        grid=(2,),
        out_shape=tuple(jax.ShapeDtypeStruct(s, t) for s, t in out),
        in_specs=in_specs,
        out_specs=out_specs,
        scratch_shapes=scratch,
        input_output_aliases=aliases,
        compiler_params=params(),
        cost_estimate=pl.CostEstimate(
            flops=6 * 10**9, transcendentals=0, bytes_accessed=10 * 10**6
        ),
        name="attention_backward",
    )(place, normed, qkv, qkv, qkv, prob, dmiddle_b, wo, *extra)


def input_kernel(seq, table, images, dmiddle, wq, dq, dk, dv, out_o, sums_o, rows_s):
    step = pl.program_id(0)
    width = table.shape[1]

    @pl.when(step == 0)
    def _():
        rows_s[...] = jnp.zeros_like(rows_s)
        sums_o[...] = jnp.zeros_like(sums_o)

    rows_s[0:seq, :] = images[0].astype(F32)
    standardized, factor = normalize(rows_s[...])
    gradient = (
        nt(dq[0], wq[:, 0:width])
        + nt(dk[0], wq[:, width : 2 * width])
        + nt(dv[0], wq[:, 2 * width : 3 * width])
    )
    out = dmiddle[0] + norm_backward(gradient, standardized, factor, table[0:1, :])
    out_o[0] = out[:seq].astype(BF16)
    sums_o[0:1, :] += jnp.sum(gradient * standardized, axis=0, keepdims=True)
    sums_o[1:2, :] += jnp.sum(gradient, axis=0, keepdims=True)


def input_gradient(table, images, dmiddle, wq, dqkv):
    count, seq, width = images.shape
    pad = dmiddle.shape[1]
    return pl.pallas_call(
        functools.partial(input_kernel, seq),
        grid=(count,),
        out_shape=(
            jax.ShapeDtypeStruct((count, seq, width), BF16),
            jax.ShapeDtypeStruct((8, width), F32),
        ),
        in_specs=[
            resident(table.shape),
            per_image((1, seq, width)),
            per_image((1, pad, width)),
            resident(wq.shape),
        ]
        + [per_image((1, pad, width))] * 3,
        out_specs=[per_image((1, seq, width)), resident((8, width))],
        scratch_shapes=[pltpu.VMEM((pad, width), F32)],
        compiler_params=params(),
        cost_estimate=pl.CostEstimate(
            flops=5 * 10**9, transcendentals=0, bytes_accessed=15 * 10**6
        ),
        name="input_gradient",
    )(table, images, dmiddle, wq, *dqkv)


def vectors_kernel(sums1, sums2, bias_a, bias_b, first, second, third, out):
    half = out.shape[2]
    for y in range(2):
        lanes = slice(y * half, (y + 1) * half)
        out[y, 0:2, :] = sums1[0:2, lanes]
        out[y, 4:8, :] = sums2[0:4, lanes]
        for n, bias in enumerate((bias_a, bias_b)):
            for m in range(2):
                row = 8 + 2 * n + m
                out[y, row : row + 1, :] = bias[y, 0:1, m * half : (m + 1) * half]
    per_half = half // LANES
    for call, sums in enumerate((first, second, third)):
        for j in range(2):
            y, at = divmod(2 * call + j, per_half)
            out[y, 2:4, at * LANES : (at + 1) * LANES] = sums[j, 0:2, :]


def vectors(sums1, sums2, bias_a, bias_b, heads):
    half = sums1.shape[1] // 2
    return pl.pallas_call(
        vectors_kernel,
        out_shape=jax.ShapeDtypeStruct((2, 12, half), F32),
        compiler_params=params(8 * 2**20),
        name="vectors",
    )(sums1, sums2, bias_a, bias_b, *heads)


def mlp_out_kernel(place, mine_0, mine_1, other_0, other_1, *refs):
    up_o, down_o = refs[-2:]
    core, across = place[1], place[2]
    rows = mine_0.shape[1]

    def write(up, down):
        @pl.loop(0, 4)
        def _(t):
            at = pl.ds(pl.multiple_of(t * rows, rows), rows)
            up_o[at, :] = up[t].astype(F32)
            down_o[at, :] = down[t].astype(F32)

    for s, (mine, other) in enumerate(((mine_0, other_0), (mine_1, other_1))):
        here = (pl.program_id(0) ^ across) == s

        @pl.when(jnp.logical_and(core == 0, here))
        def _():
            write(mine, other)

        @pl.when(jnp.logical_and(core == 1, here))
        def _():
            write(other, mine)


def mlp_out(part, place, pieces, earlier):
    _, rows, block = pieces[0].shape
    width = rows * 8
    shapes = (
        jax.ShapeDtypeStruct((width // 2, 4 * block), F32),
        jax.ShapeDtypeStruct((2 * block, width), F32),
    )
    return pl.pallas_call(
        mlp_out_kernel,
        grid=(2,),
        in_specs=[SMEM] + [resident(p.shape) for p in pieces] + [ANY] * len(earlier),
        out_specs=[
            pl.BlockSpec((width // 2, block), lambda x: (0, 2 * x + part)),
            pl.BlockSpec((block // 2, width), lambda x: (2 * part + x, 0)),
        ],
        out_shape=shapes,
        input_output_aliases={5 + n: n for n in range(len(earlier))},
        compiler_params=params(32 * 2**20),
        name="mlp_out",
    )(place, *pieces, *earlier)


def attention_out_kernel(place, *refs):
    large, small, (qkv_o, out_o) = refs[:4], refs[4:8], refs[8:]
    core, across = place[1], place[2]
    width = out_o.shape[1]
    half = width // 2
    size = half // 8

    def write(s):
        for n in range(2):
            owner = core ^ n
            first, second = large[2 * n + s], small[2 * n + s]

            @pl.loop(0, 4)
            def _(t):
                rows = pl.ds(pl.multiple_of(t * size, size), size)
                for call in range(3):
                    value = second[t] if call == 2 else first[t, call * size : (call + 1) * size]
                    value = value.astype(F32)
                    for c in range(3):
                        col = (2 * call + owner) * LANES + c * width
                        cols = pl.ds(pl.multiple_of(col, LANES), LANES)
                        qkv_o[rows, cols] = value[:, c * LANES : (c + 1) * LANES]
                cols = pl.ds(pl.multiple_of(owner * half, half), half)
                out_o[rows, cols] = first[t, 2 * size : 3 * size].astype(F32)

    for s in range(2):

        @pl.when((pl.program_id(0) ^ across) == s)
        def _():
            write(s)


def attention_out(place, pieces, width):
    shapes = ((width // 2, 3 * width), (width // 2, width))
    return pl.pallas_call(
        attention_out_kernel,
        grid=(2,),
        out_shape=tuple(jax.ShapeDtypeStruct(s, F32) for s in shapes),
        in_specs=[SMEM] + [resident(p.shape) for p in pieces],
        out_specs=[pl.BlockSpec((width // 4, s[1]), lambda x: (x, 0)) for s in shapes],
        compiler_params=params(32 * 2**20),
        name="attention_out",
    )(place, *pieces)


def sum_kernel(parts, *refs):
    inputs, outputs = refs[: len(refs) - parts], refs[len(refs) - parts :]
    rows = 48 if outputs[0].shape[0] % 48 == 0 else outputs[0].shape[0]

    @pl.loop(0, outputs[0].shape[0] // rows)
    def _(i):
        at = pl.ds(pl.multiple_of(i * rows, rows), rows)
        for n, out in enumerate(outputs):
            total = inputs[0][n, at].astype(F32)
            for value in inputs[1:]:
                total = total + value[n, at].astype(F32)
            out[at, :] = total.astype(BF16)


def sum_parts(arrays, parts, steps):
    _, rows, cols = arrays[0].shape
    return pl.pallas_call(
        functools.partial(sum_kernel, parts),
        grid=(steps,),
        in_specs=[pl.BlockSpec((parts, rows // steps, cols), lambda i: (0, i, 0))] * len(arrays),
        out_specs=[pl.BlockSpec((rows // steps, cols), lambda i: (i, 0))] * parts,
        out_shape=[jax.ShapeDtypeStruct((rows, cols), BF16)] * parts,
        compiler_params=params(24 * 2**20),
        name="sum_parts",
    )(*arrays)


def sum_depths_kernel(place, kept, received, *outputs):
    for n, out in enumerate(outputs):
        at = place[3] ^ n
        out[...] = (kept[at].astype(F32) + received[at].astype(F32)).astype(BF16)


def sum_depths(place, kept, received):
    return pl.pallas_call(
        sum_depths_kernel,
        in_specs=[SMEM] + [pl.BlockSpec(memory_space=pltpu.VMEM)] * 2,
        out_shape=[jax.ShapeDtypeStruct(kept.shape[1:], BF16)] * 4,
        compiler_params=params(24 * 2**20),
        name="sum_depths",
    )(place, kept, received)


def stack_kernel(place, *refs):
    for n, ref in enumerate(refs[:-1]):
        refs[-1][place[3] ^ n] = ref[...]


def stack(place, arrays):
    return pl.pallas_call(
        stack_kernel,
        in_specs=[SMEM] + [pl.BlockSpec(memory_space=pltpu.VMEM)] * len(arrays),
        out_shape=jax.ShapeDtypeStruct((len(arrays),) + arrays[0].shape, BF16),
        compiler_params=params(24 * 2**20),
        name="stack",
    )(place, *arrays)


def swap(array, axis, step):
    size = lax.axis_size(axis)
    return lax.ppermute(array, axis, [(i, i ^ step) for i in range(size)])


def turn(array, order):
    pairs = []
    for r in range(lax.axis_size("rep")):
        for s in range(2):
            there = 2 * r + (s ^ 1) if (r & 1) == order else 2 * (r ^ 2) + s
            pairs.append((2 * r + s, there))
    return lax.ppermute(array, ("rep", "shard"), pairs)


def pick(array, index, axis=0):
    return lax.dynamic_index_in_dim(array, index, axis, keepdims=False)


DEPTHS = (8, 4, 12)


def reduce_pieces(place, keep, send):
    rows, cols = keep.shape[3:]
    got = swap(send.reshape(2, 8 * rows, cols), "rep", 1)
    now, away = sum_parts((keep.reshape(2, 8 * rows, cols), got), 2, 4)
    got = turn(away, 0)
    now, away = sum_parts([a.reshape(2, 4 * rows, cols) for a in (now, got)], 2, 2)
    got = turn(away, 1)
    now, *away = sum_depths(place, now.reshape(4, rows, cols), got.reshape(4, rows, cols))
    got = [swap(part, "rep", step) for part, step in zip(away, DEPTHS)]
    (now,) = sum_parts([a.reshape(1, rows, cols) for a in [now] + got], 1, 1)
    step = 16
    while step < lax.axis_size("rep"):
        pair = [a.reshape(1, rows, cols) for a in (now, swap(now, "rep", step))]
        (now,) = sum_parts(pair, 1, 1)
        step *= 2
    got = [swap(now, "rep", step) for step in DEPTHS]
    mine = stack(place, [now] + got)
    near = swap(mine, "rep", 2)
    other = swap(mine, "rep", 1)
    return mine, near, other, swap(near, "rep", 1)


def reduce_vectors(whole, side):
    now = whole
    step = 1
    while step < lax.axis_size("rep"):
        now = now + swap(now, "rep", step)
        step *= 2
    other = swap(pick(now, 1 - side), "shard", 1)
    return pick(now, side) + other


def per_device(
    images,
    ln1_gain,
    first_norm_bias,
    qkv_weight,
    q_bias,
    v_bias,
    out_weight,
    out_bias,
    ln2_gain,
    second_norm_bias,
    up_weight,
    up_bias,
    down_weight,
    down_bias,
    cotangent,
):
    count, seq, width = images.shape
    head = width // HEADS
    pad = -(-seq // 16) * 16
    tokens = count * pad
    half = width // 2
    index = lax.axis_index("rep")
    side = lax.axis_index("shard")
    core = index & 1
    across = (index >> 1) & 1
    depth = ((index >> 2) & 1) * 2 + ((index >> 3) & 1)
    place = jnp.stack([side, core, across, depth]).astype(jnp.int32)

    small = jnp.concatenate(
        [
            ln1_gain, first_norm_bias, q_bias, v_bias, out_bias, ln2_gain, second_norm_bias,
            down_bias, up_bias,
        ]
    ).reshape(-1, half)
    small_other = swap(small, "shard", 1)
    first = jnp.concatenate(
        [
            pick(qkv_weight.reshape(2, half // 2, -1), core),
            pick(out_weight.reshape(2, half // 2, -1), core),
        ],
        axis=1,
    )
    first_a = swap(first, "shard", 1)
    first_b = swap(first_a, "rep", 1)
    low = jnp.where(side == 0, small, small_other)
    high = jnp.where(side == 0, small_other, small)
    table = jnp.concatenate([low, high], axis=1).astype(F32)

    block = up_weight.shape[1] // 4
    waves = []
    for part in range(2):
        ups = [
            pick(up_weight[:, c * block : (c + 1) * block].reshape(2, half // 2, block), core)
            for c in (part, 2 + part)
        ]
        rows = down_weight[part * block : (part + 1) * block].reshape(2, block // 2, width)
        mine = jnp.concatenate(ups + [pick(rows, core)], axis=0)
        wave_a = swap(mine, "shard", 1)
        waves.append((up_weight, down_weight, wave_a, swap(wave_a, "rep", 1)))

    flat = lambda a: a.reshape(tokens, -1)
    deep = lambda a: a.reshape(count, pad, -1)
    normed, qkv, prob, context, middle, normed2, padded, wq, wo = attention_forward(
        place, images, cotangent, table, (qkv_weight, out_weight, first_a, first_b), pad, head
    )
    normed2, middle, padded = flat(normed2), flat(middle), flat(padded)
    keep, send, bias_a, r_acc, d_acc = mlp(
        0, place, normed2, padded, table, waves[0], middle, (), count, seq
    )
    mlp_a = reduce_pieces(place, keep, send)
    keep, send, bias_b, result, dmiddle, dmiddle_b, sums2 = mlp(
        1, place, normed2, padded, table, waves[1], middle, (r_acc, d_acc), count, seq
    )
    mlp_b = reduce_pieces(place, keep, send)
    normed, qkv, context = flat(normed), flat(qkv), flat(context)
    heads = []
    dqkv = kept = None
    for call in range(3):
        *kept, dq, dk, dv, sums = attention_backward(
            call, place, normed, qkv, prob, dmiddle_b, wo, context, kept, dqkv, head
        )
        dqkv = (dq, dk, dv)
        heads.append(sums)
        if call == 1:
            attn = reduce_pieces(place, *kept)
    attn += reduce_pieces(place, *kept)
    grad_images, sums1 = input_gradient(table, images, deep(dmiddle), wq, [deep(d) for d in dqkv])
    partial = vectors(sums1, sums2, bias_a, bias_b, heads)

    outs = mlp_out(0, place, mlp_a, ())
    p_up, p_down = mlp_out(1, place, mlp_b, outs)
    p_qkv, p_out = attention_out(place, attn, width)

    rows = reduce_vectors(partial, side)
    return (
        result,
        grad_images,
        rows[0],
        rows[1],
        p_qkv,
        rows[2],
        rows[3],
        p_out,
        rows[6],
        rows[4],
        rows[5],
        p_up,
        rows[8:].reshape(-1),
        p_down,
        rows[7],
    )


def solution(mesh):
    in_specs = (
        P(("rep", "shard"), None, None),
        P("shard"),
        P("shard"),
        P("shard", None),
        P("shard"),
        P("shard"),
        P("shard", None),
        P("shard"),
        P("shard"),
        P("shard"),
        P("shard", None),
        P("shard"),
        P("shard", None),
        P("shard"),
        P(("rep", "shard"), None, None),
    )
    out_specs = (
        P(("rep", "shard"), None, None),
        P(("rep", "shard"), None, None),
        P("shard"),
        P("shard"),
        P("shard", None),
        P("shard"),
        P("shard"),
        P("shard", None),
        P("shard"),
        P("shard"),
        P("shard"),
        P("shard", None),
        P("shard"),
        P("shard", None),
        P("shard"),
    )

    return jax.shard_map(
        per_device, mesh=mesh, in_specs=in_specs, out_specs=out_specs, check_vma=False
    )
```
